512 devices in a mesh: row: 32 (over z, x_lo, core), col: 16 (over y, x_hi).
Axes of the slice: x: 4 (x_hi: 2, x_lo: 2; x = x_hi * 2 + x_lo), y: 8, z: 8, core: 2. Of those that a mesh axis runs over, the one named last changes fastest.
Arguments:
- amplitudes: float32 [8192, 8192], P('row', 'col'), may hold values from -6 to 6
- factor: float32 [8192, 512], P('col'), may hold values from -1.2 to 1.2
- denominators: float32 [8192, 8192], P('row', 'col'), may hold values from 1 to 4
Outputs:
- new_amplitudes: float32 [8192, 8192], P('row', 'col')
The draws below stay inside these ranges and needn't reach their ends.
All inputs are finite; a program needn't handle non-finite values.
Results may differ from the reference program's by a relative error of at most 0.0001.
Values sent between devices are 32-bit elements; how exact they have to be, the bound alone decides.
No kernel may reach another device: no remote copies, remote signals or barrier semaphores. Data moves between devices by JAX's collectives and lax.ppermute only.
A program may use at most 64 MiB of HBM per device.

```python
import math
import jax
import jax.numpy as jnp
from jax import lax

K = 512
ITERS = 2
NT = 8192


def shard_levels(key, dims, cuts, low, top_value):
    gain, own = 1.0, jax.random.fold_in(key, 6)
    for position, blocks in cuts:
        heights = jnp.exp(jax.random.uniform(jax.random.fold_in(own, position), (blocks,), jnp.float32, low / len(cuts), top_value / len(cuts)))
        gain = gain * jnp.repeat(heights, dims[position] // blocks).reshape([-1 if axis == position else 1 for axis in range(len(dims))])
    return gain


def gaussian(stream_key, shape, deviation, most, split=(), dtype=jnp.bfloat16):
    array = jax.random.normal(stream_key, shape, jnp.float32) * deviation
    if len(split) > 0:
        array = shard_levels(stream_key, shape, split, -0.22, 0.18) * array
    return jnp.clip(array, min=-most, max=most).astype(dtype)


def setup_inputs(seed: int = 0) -> dict:
    streams_of = jax.random.split(jax.random.key(seed), 4)
    return {
        "amplitudes": gaussian(streams_of[0], (NT, NT), 1.0, 6.0, ((0, 32), (1, 16)), jnp.float32),
        "factor": gaussian(streams_of[1], (NT, K), 0.2, 1.2, ((0, 16),), jnp.float32),
        "denominators": jnp.clip(jnp.exp(math.log(4.0) - 1.3862944 * jax.random.uniform(streams_of[2], (NT, NT), jnp.float32) ** shard_levels(streams_of[2], (NT, NT), ((0, 32), (1, 16)), -0.2, 0.2)), 1.0, 4.0),
    }


def reference(amplitudes, factor, denominators):
    high = lax.Precision.HIGHEST
    scale = 1.0 / math.sqrt(NT)
    base = jnp.dot(factor, factor.T, precision=high)
    amp = amplitudes
    for step in range(ITERS):
        ymat = jnp.dot(amp, factor, precision=high) * scale
        mixed = jnp.dot(ymat, factor.T, precision=high)
        result = base + jnp.dot(ymat, ymat.T, precision=high) + mixed + mixed.T
        amp = result / denominators
    return amp
```

```python
import math

import jax
import jax.numpy as jnp
from jax import lax
from jax.sharding import PartitionSpec as P

ITERS = 2
PRECISION = lax.Precision.HIGH


def spread(block, axis, groups=None):
    return lax.all_to_all(block, axis, split_axis=0, concat_axis=0, axis_index_groups=groups, tiled=True)


def local(amplitudes, factor, denominators):
    rows, depth = amplitudes.shape[0], factor.shape[1]
    nrow = lax.axis_size("row")
    ncol = lax.axis_size("col")
    ratio = nrow // ncol
    here_row = lax.axis_index("row")
    here_col = lax.axis_index("col")
    scale = 1.0 / math.sqrt(rows * nrow)
    mine = lax.dynamic_slice_in_dim(factor, here_row % ratio * rows, rows, 0)
    mine = jnp.where(here_row // ratio == here_col, mine, 0.0)
    apart = [[k * ratio + e for k in range(ncol)] for e in range(ratio)]
    team = [[k * ratio + e for e in range(ratio)] for k in range(ncol)]
    turn = []
    for k in range(ncol):
        for e in range(ratio):
            for c in range(ncol):
                turn.append(((k * ratio + e) * ncol + c, (c * ratio + e) * ncol + k))
    amp = amplitudes
    for step in range(ITERS):
        part = jnp.dot(amp, factor, precision=PRECISION) * scale + mine
        terms = spread(part, "col")
        piece = terms.reshape(ncol, rows // ncol, depth).sum(0)
        turned = lax.ppermute(piece, ("row", "col"), turn)
        z_rows = spread(jnp.tile(piece, (ncol, 1)), "col")
        turned, z_rows = lax.optimization_barrier((turned, z_rows))
        z_half = spread(jnp.tile(turned, (ncol, 1)), "row", apart)
        z_cols = spread(jnp.tile(z_half, (ratio, 1)), "row", team)
        full = lax.dot_general(z_rows, z_cols, (((1,), (1,)), ((), ())), precision=PRECISION)
        amp = full / denominators
    return amp


def solution(mesh):
    return jax.shard_map(
        local,
        mesh=mesh,
        in_specs=(P("row", "col"), P("col", None), P("row", "col")),
        out_specs=P("row", "col"),
        check_vma=False,
    )
```

```python
import math

import jax
import jax.numpy as jnp
from jax import lax
from jax.sharding import PartitionSpec as P

ITERS = 2
PRECISION = lax.Precision.HIGH
PAIR = 2
CORES = 2


def spread(block, axis, groups):
    return lax.all_to_all(block, axis, split_axis=0, concat_axis=0, axis_index_groups=groups, tiled=True)


def ordered(first, second, swapped):
    return jnp.where(swapped, jnp.concatenate([second, first]), jnp.concatenate([first, second]))


def local(amplitudes, factor, denominators):
    rows, depth = amplitudes.shape[0], factor.shape[1]
    nrow = lax.axis_size("row")
    ncol = lax.axis_size("col")
    line = ncol // PAIR
    here_row = lax.axis_index("row")
    here_col = lax.axis_index("col")
    scale = 1.0 / math.sqrt(rows * nrow)
    mine = lax.dynamic_slice_in_dim(factor, here_row % CORES * rows, rows, 0)
    mine = jnp.where(here_row // CORES == here_col, mine, 0.0)
    along_y = [[y * PAIR + u for y in range(line)] for u in range(PAIR)]
    along_z = [[z * PAIR * CORES + q for z in range(line)] for q in range(PAIR * CORES)]
    team = [[k * CORES + e for e in range(CORES)] for k in range(nrow // CORES)]
    across = [(c, c ^ 1) for c in range(ncol)]
    turns = [[], []]
    for r in range(nrow):
        for c in range(ncol):
            j = c % PAIR * line + c // PAIR
            for t in range(PAIR):
                to = (j // PAIR * PAIR + (j % PAIR ^ t)) * CORES + r % CORES
                turns[t].append((r * ncol + c, to * ncol + r // CORES))
    odd_u = here_col % PAIR == 1
    odd_v = here_row // CORES % PAIR == 1
    amp = amplitudes
    for step in range(ITERS):
        part = jnp.dot(amp, factor, precision=PRECISION) * scale + mine
        terms = spread(part, "col", [sum(along_y, [])])
        piece = terms.reshape(ncol, rows // ncol, depth).sum(0)
        near = lax.ppermute(piece, ("row", "col"), turns[0])
        far = lax.ppermute(piece, ("row", "col"), turns[1])
        row_half = spread(jnp.tile(piece, (line, 1)), "col", along_y)
        row_rest = lax.ppermute(row_half, "col", across)
        two = ordered(near, far, odd_v)
        col_half = spread(jnp.tile(two, (line, 1)), "row", along_z)
        z_cols = spread(jnp.tile(col_half, (CORES, 1)), "row", team)
        z_rows = ordered(row_half, row_rest, odd_u)
        full = lax.dot_general(z_rows, z_cols, (((1,), (1,)), ((), ())), precision=PRECISION)
        amp = full / denominators
    return amp


def solution(mesh):
    return jax.shard_map(
        local,
        mesh=mesh,
        in_specs=(P("row", "col"), P("col", None), P("row", "col")),
        out_specs=P("row", "col"),
        check_vma=False,
    )
```

```python
import math

import jax
import jax.numpy as jnp
from jax import lax
from jax.sharding import PartitionSpec as P

ITERS = 2
PRECISION = lax.Precision.HIGH
PAIR = 2
CORES = 2


def spread(block, axis, groups):
    return lax.all_to_all(block, axis, split_axis=0, concat_axis=0, axis_index_groups=groups, tiled=True)


def ordered(first, second, swapped):
    return jnp.where(swapped, jnp.concatenate([second, first]), jnp.concatenate([first, second]))


def local(amplitudes, factor, denominators):
    rows, depth = amplitudes.shape[0], factor.shape[1]
    nrow = lax.axis_size("row")
    ncol = lax.axis_size("col")
    line = ncol // PAIR
    here_row = lax.axis_index("row")
    here_col = lax.axis_index("col")
    scale = 1.0 / math.sqrt(rows * nrow)
    mine = lax.dynamic_slice_in_dim(factor, here_row % CORES * rows, rows, 0)
    mine = jnp.where(here_row // CORES == here_col, mine, 0.0)
    along_y = [[y * PAIR + u for y in range(line)] for u in range(PAIR)]
    across = [(c, c ^ 1) for c in range(ncol)]
    partner = [(r, r ^ 1) for r in range(nrow)]
    turn = []
    along_zv = [[] for _ in range(CORES)]
    for u in range(PAIR):
        for y in range(line):
            place = (y + line // 2) % line * PAIR + u
            for e in range(CORES):
                along_zv[e].append(place * CORES + e)
            for r in range(nrow):
                turn.append((r * ncol + y * PAIR + u, (place * CORES + r % CORES) * ncol + r // CORES))
    odd_u = here_col % PAIR == 1
    odd_e = here_row % CORES == 1
    amp = amplitudes
    for _ in range(ITERS):
        part = jnp.dot(amp, factor, precision=PRECISION) * scale + mine
        terms = spread(part, "col", [sum(along_y, [])])
        piece = terms.reshape(ncol, rows // ncol, depth).sum(0)
        turned = lax.ppermute(piece, ("row", "col"), turn)
        row_half = spread(jnp.tile(piece, (line, 1)), "col", along_y)
        row_rest = lax.ppermute(row_half, "col", across)
        col_half = spread(jnp.tile(turned, (ncol, 1)), "row", along_zv)
        col_rest = lax.ppermute(col_half, "row", partner)
        z_cols = ordered(col_half, col_rest, odd_e)
        z_rows = ordered(row_half, row_rest, odd_u)
        full = lax.dot_general(z_rows, z_cols, (((1,), (1,)), ((), ())), precision=PRECISION)
        amp = full / denominators
    return amp


def solution(mesh):
    return jax.shard_map(
        local,
        mesh=mesh,
        in_specs=(P("row", "col"), P("col", None), P("row", "col")),
        out_specs=P("row", "col"),
        check_vma=False,
    )
```

```python
import math

import jax
import jax.numpy as jnp
from jax import lax
from jax.sharding import PartitionSpec as P

ITERS = 2
PRECISION = lax.Precision.HIGH
PAIR = 2
CORES = 2


def spread(block, axis, groups):
    return lax.all_to_all(block, axis, split_axis=0, concat_axis=0, axis_index_groups=groups, tiled=True)


def ordered(first, second, swapped):
    return jnp.where(swapped, jnp.concatenate([second, first]), jnp.concatenate([first, second]))


def local(amplitudes, factor, denominators):
    rows, depth = amplitudes.shape[0], factor.shape[1]
    nrow = lax.axis_size("row")
    ncol = lax.axis_size("col")
    line = ncol // PAIR
    here_row = lax.axis_index("row")
    here_col = lax.axis_index("col")
    scale = 1.0 / math.sqrt(rows * nrow)
    mine = lax.dynamic_slice_in_dim(factor, here_row % CORES * rows, rows, 0)
    mine = jnp.where(here_row // CORES == here_col, mine, 0.0)
    along_y = [[y * PAIR + u for y in range(line)] for u in range(PAIR)]
    across = [(c, c ^ 1) for c in range(ncol)]
    partner = [(r, r ^ 1) for r in range(nrow)]
    turn = []
    along_zv = [[] for _ in range(CORES)]
    for u in range(PAIR):
        for y in range(line):
            place = (y + line // 2) % line * PAIR + u
            for e in range(CORES):
                along_zv[e].append(place * CORES + e)
            for r in range(nrow):
                turn.append((r * ncol + y * PAIR + u, (place * CORES + r % CORES) * ncol + r // CORES))
    odd_u = here_col % PAIR == 1
    odd_e = here_row % CORES == 1
    amp = amplitudes
    for _ in range(ITERS):
        part = jnp.dot(amp, factor, precision=PRECISION) * scale + mine
        terms = spread(part, "col", [sum(along_y, [])])
        piece = terms.reshape(ncol, rows // ncol, depth).sum(0)
        row_half = spread(jnp.tile(piece, (line, 1)), "col", along_y)
        turned = lax.ppermute(piece, ("row", "col"), turn)
        copies = jnp.tile(turned, (ncol, 1))
        col_half = spread(copies, "row", along_zv)
        row_rest = lax.ppermute(row_half, "col", across)
        z_rows = lax.optimization_barrier(ordered(row_half, row_rest, odd_u))
        col_rest = lax.ppermute(col_half, "row", partner)
        z_cols = ordered(col_half, col_rest, odd_e)
        full = lax.dot_general(z_rows, z_cols, (((1,), (1,)), ((), ())), precision=PRECISION)
        amp = full / denominators
    return amp


def solution(mesh):
    return jax.shard_map(
        local,
        mesh=mesh,
        in_specs=(P("row", "col"), P("col", None), P("row", "col")),
        out_specs=P("row", "col"),
        check_vma=False,
    )
```

```python
import math

import jax
import jax.numpy as jnp
from jax import lax
from jax.sharding import PartitionSpec as P

ITERS = 2
PRECISION = lax.Precision.HIGH
PAIR = 2
CORES = 2


def spread(block, axis, groups):
    return lax.all_to_all(block, axis, split_axis=0, concat_axis=0, axis_index_groups=groups, tiled=True)


def ordered(first, second, swapped):
    return jnp.where(swapped, jnp.concatenate([second, first]), jnp.concatenate([first, second]))


def local(amplitudes, factor, denominators):
    rows, depth = amplitudes.shape[0], factor.shape[1]
    nrow = lax.axis_size("row")
    ncol = lax.axis_size("col")
    line = ncol // PAIR
    here_row = lax.axis_index("row")
    here_col = lax.axis_index("col")
    scale = 1.0 / math.sqrt(rows * nrow)
    mine = lax.dynamic_slice_in_dim(factor, here_row % CORES * rows, rows, 0)
    mine = jnp.where(here_row // CORES == here_col, mine, 0.0)
    partner = [(r, r ^ 1) for r in range(nrow)]
    turn = []
    along_zv = [[] for _ in range(CORES)]
    for c in range(ncol):
        place = (c // PAIR + line // 2) % line * PAIR + c % PAIR
        for e in range(CORES):
            along_zv[e].append(place * CORES + e)
        for r in range(nrow):
            turn.append((r * ncol + c, (place * CORES + r % CORES) * ncol + r // CORES))
    odd_e = here_row % CORES == 1
    amp = amplitudes
    for _ in range(ITERS):
        part = jnp.dot(amp, factor, precision=PRECISION) * scale + mine
        terms = spread(part, "col", None)
        piece = terms.reshape(ncol, rows // ncol, depth).sum(0)
        z_rows = spread(jnp.tile(piece, (ncol, 1)), "col", None)
        turned = lax.ppermute(piece, ("row", "col"), turn)
        copies = jnp.tile(turned, (ncol, 1))
        col_half = spread(copies, "row", along_zv)
        col_rest = lax.ppermute(col_half, "row", partner)
        z_cols = ordered(col_half, col_rest, odd_e)
        full = lax.dot_general(z_rows, z_cols, (((1,), (1,)), ((), ())), precision=PRECISION)
        amp = full / denominators
    return amp


def solution(mesh):
    return jax.shard_map(
        local,
        mesh=mesh,
        in_specs=(P("row", "col"), P("col", None), P("row", "col")),
        out_specs=P("row", "col"),
        check_vma=False,
    )
```

```python
import math

import jax
import jax.numpy as jnp
from jax import lax
from jax.sharding import PartitionSpec as P

ITERS = 2
PRECISION = lax.Precision.HIGH
PAIR = 2
CORES = 2


def spread(block, axis, groups):
    return lax.all_to_all(block, axis, split_axis=0, concat_axis=0, axis_index_groups=groups, tiled=True)


def ordered(first, second, swapped):
    return jnp.where(swapped, jnp.concatenate([second, first]), jnp.concatenate([first, second]))


def local(amplitudes, factor, denominators):
    rows, depth = amplitudes.shape[0], factor.shape[1]
    nrow = lax.axis_size("row")
    ncol = lax.axis_size("col")
    line = ncol // PAIR
    here_row = lax.axis_index("row")
    here_col = lax.axis_index("col")
    scale = 1.0 / math.sqrt(rows * nrow)
    mine = lax.dynamic_slice_in_dim(factor, here_row % CORES * rows, rows, 0)
    mine = jnp.where(here_row // CORES == here_col, mine, 0.0)
    partner = [(r, r ^ 1) for r in range(nrow)]
    along_yu = [[y * PAIR + u for u in range(PAIR) for y in range(line)]]
    turn = []
    along_zv = [[] for _ in range(CORES)]
    for c in along_yu[0]:
        place = (c // PAIR + line // 2) % line * PAIR + c % PAIR
        for e in range(CORES):
            along_zv[e].append(place * CORES + e)
        for r in range(nrow):
            turn.append((r * ncol + c, (place * CORES + r % CORES) * ncol + r // CORES))
    odd_e = here_row % CORES == 1
    amp = amplitudes
    for _ in range(ITERS):
        part = jnp.dot(amp, factor, precision=PRECISION) * scale + mine
        terms = spread(part, "col", along_yu)
        piece = terms.reshape(ncol, rows // ncol, depth).sum(0)
        z_rows = spread(jnp.tile(piece, (ncol, 1)), "col", along_yu)
        turned = lax.ppermute(piece, ("row", "col"), turn)
        copies = jnp.tile(turned, (ncol, 1))
        col_half = spread(copies, "row", along_zv)
        col_rest = lax.ppermute(col_half, "row", partner)
        z_cols = ordered(col_half, col_rest, odd_e)
        full = lax.dot_general(z_rows, z_cols, (((1,), (1,)), ((), ())), precision=PRECISION)
        amp = full / denominators
    return amp


def solution(mesh):
    return jax.shard_map(
        local,
        mesh=mesh,
        in_specs=(P("row", "col"), P("col", None), P("row", "col")),
        out_specs=P("row", "col"),
        check_vma=False,
    )
```

```python
import math

import jax
import jax.numpy as jnp
from jax import lax
from jax.sharding import PartitionSpec as P

ITERS = 2
PRECISION = lax.Precision.HIGH
PAIR = 2
CORES = 2


def spread(block, axis, groups):
    return lax.all_to_all(block, axis, split_axis=0, concat_axis=0, axis_index_groups=groups, tiled=True)


def local(amplitudes, factor, denominators):
    rows, depth = amplitudes.shape[0], factor.shape[1]
    nrow = lax.axis_size("row")
    ncol = lax.axis_size("col")
    line = ncol // PAIR
    thin = rows // ncol
    here_row = lax.axis_index("row")
    here_col = lax.axis_index("col")
    first = here_row % CORES == 0
    scale = 1.0 / math.sqrt(rows * nrow)
    mine = lax.dynamic_slice_in_dim(factor, here_row % CORES * rows, rows, 0)
    mine = jnp.where(here_row // CORES == here_col, mine, 0.0)
    team = [[k * CORES + e for e in range(CORES)] for k in range(ncol)]
    partner = [(r, r ^ 1) for r in range(nrow)]
    order = [y * PAIR + u for u in range(PAIR) for y in range(line)]
    place = [(c // PAIR + line // 2) % line * PAIR + c % PAIR for c in order]
    turn = []
    for c, q in zip(order, place):
        for k in range(ncol):
            turn.append(((k * CORES + 1) * ncol + c, (q * CORES + 1) * ncol + k))
    both = [[k * CORES * ncol + c for c in order] for k in range(ncol)]
    both += [[(q * CORES + 1) * ncol + c for q in place] for c in range(ncol)]
    amp = amplitudes
    for step in range(ITERS):
        part = jnp.dot(amp, factor, precision=PRECISION) * scale + mine
        terms = spread(part, "col", [order])
        piece = terms.reshape(ncol, thin, depth).sum(0)
        pieces = lax.all_gather(piece, "row", axis=0, axis_index_groups=team, tiled=True)
        turned = lax.ppermute(pieces, ("row", "col"), turn)
        own = jnp.where(first, pieces, turned)
        got = spread(jnp.tile(own, (ncol, 1)), ("row", "col"), both)
        other = lax.ppermute(got, "row", partner)
        got = got.reshape(ncol, CORES, thin, depth)
        other = other.reshape(ncol, CORES, thin, depth)
        z_rows = jnp.where(first, got[:, 0], other[:, 1]).reshape(rows, depth)
        z_cols = jnp.where(first, other, got).transpose(1, 0, 2, 3).reshape(CORES * rows, depth)
        full = lax.dot_general(z_rows, z_cols, (((1,), (1,)), ((), ())), precision=PRECISION)
        amp = full / denominators
    return amp


def solution(mesh):
    return jax.shard_map(
        local,
        mesh=mesh,
        in_specs=(P("row", "col"), P("col", None), P("row", "col")),
        out_specs=P("row", "col"),
        check_vma=False,
    )
```

```python
import math

import jax
import jax.numpy as jnp
from jax import lax
from jax.sharding import PartitionSpec as P

ITERS = 2
PRECISION = lax.Precision.HIGH
PAIR = 2
CORES = 2


def spread(block, axis, groups):
    return lax.all_to_all(block, axis, split_axis=0, concat_axis=0, axis_index_groups=groups, tiled=True)


def local(amplitudes, factor, denominators):
    rows, depth = amplitudes.shape[0], factor.shape[1]
    nrow = lax.axis_size("row")
    ncol = lax.axis_size("col")
    line = ncol // PAIR
    thin = rows // ncol
    here_row = lax.axis_index("row")
    here_col = lax.axis_index("col")
    first = here_row % CORES == 0
    scale = 1.0 / math.sqrt(rows * nrow)
    mine = lax.dynamic_slice_in_dim(factor, here_row % CORES * rows, rows, 0)
    mine = jnp.where(here_row // CORES == here_col, mine, 0.0)
    team = [[k * CORES + e for e in range(CORES)] for k in range(ncol)]
    partner = [(r, r ^ 1) for r in range(nrow)]
    order = [y * PAIR + u for u in range(PAIR) for y in range(line)]
    place = [(c // PAIR + line // 2) % line * PAIR + c % PAIR for c in order]
    turn = [[] for _ in range(CORES)]
    for e in range(CORES):
        for c, q in zip(order, place):
            for k in range(ncol):
                turn[e].append(((k * CORES + e) * ncol + c, (q * CORES + 1) * ncol + k))
    both = [[k * CORES * ncol + c for c in order] for k in range(ncol)]
    both += [[(q * CORES + 1) * ncol + c for q in place] for c in range(ncol)]
    amp = amplitudes
    for _ in range(ITERS):
        part = jnp.dot(amp, factor, precision=PRECISION) * scale + mine
        terms = spread(part, "col", [order])
        piece = terms.reshape(ncol, thin, depth).sum(0)
        turned = []
        for e in range(CORES):
            turned.append(lax.ppermute(piece, ("row", "col"), turn[e]))
        pieces = lax.all_gather(piece, "row", axis=0, axis_index_groups=team, tiled=True)
        own = jnp.where(first, pieces, jnp.concatenate(turned))
        got = spread(jnp.tile(own, (ncol, 1)), ("row", "col"), both)
        other = lax.ppermute(got, "row", partner)
        got = got.reshape(ncol, CORES, thin, depth)
        other = other.reshape(ncol, CORES, thin, depth)
        z_rows = jnp.where(first, got[:, 0], other[:, 1]).reshape(rows, depth)
        z_cols = jnp.where(first, other, got).transpose(1, 0, 2, 3).reshape(CORES * rows, depth)
        full = lax.dot_general(z_rows, z_cols, (((1,), (1,)), ((), ())), precision=PRECISION)
        amp = full / denominators
    return amp


def solution(mesh):
    return jax.shard_map(
        local,
        mesh=mesh,
        in_specs=(P("row", "col"), P("col", None), P("row", "col")),
        out_specs=P("row", "col"),
        check_vma=False,
    )
```

```python
import math

import jax
import jax.numpy as jnp
from jax import lax
from jax.experimental import pallas as pl
from jax.experimental.pallas import tpu as pltpu
from jax.sharding import PartitionSpec as P

ITERS = 2
WIDE = 256
PAIR = 2
CORES = 2


def spread(block, axis, groups):
    return lax.all_to_all(block, axis, split_axis=0, concat_axis=0, axis_index_groups=groups, tiled=True)


def halves(x):
    high = x.astype(jnp.bfloat16)
    return high, (x - high.astype(jnp.float32)).astype(jnp.bfloat16)


def product(left, right, transposed):
    dims = (((1,), (1 if transposed else 0,)), ((), ()))

    def dot(a, b):
        return lax.dot_general(a, b, dims, preferred_element_type=jnp.float32)

    return dot(left[0], right[0]) + (dot(left[0], right[1]) + dot(left[1], right[0]))


def middle_kernel(scale, last, info, got, other, den, factor, out, rh, rl, ch, cl, ah, al):
    rows, thin = out.shape[0], got.shape[2]

    def sort(cols, mine, e):
        for j in range(got.shape[0]):
            here = slice(j * thin, (j + 1) * thin)
            rh[here, :], rl[here, :] = halves(mine[j, e])
            for f in range(CORES):
                there = slice(f * rows + j * thin, f * rows + (j + 1) * thin)
                ch[there, :], cl[there, :] = halves(cols[j, f])

    @pl.when(info[0] == 0)
    def _():
        sort(other, got, 0)

    @pl.when(info[0] == 1)
    def _():
        sort(got, other, 1)

    left = rh[...], rl[...]
    for at in range(0, ch.shape[0], WIDE):
        cols = slice(at, at + WIDE)
        amp = product(left, (ch[cols, :], cl[cols, :]), True) / den[:, cols]
        if last:
            out[:, cols] = amp
        else:
            ah[:, cols], al[:, cols] = halves(amp)
    if not last:
        left = ah[...], al[...]
        for at in range(0, out.shape[1], WIDE):
            cols = slice(at, at + WIDE)
            out[:, cols] = product(left, halves(factor[:, cols]), False) * scale

        @pl.when(info[1] == 1)
        def _():
            out[...] += factor[pl.ds(pl.multiple_of(info[0] * rows, rows), rows), :]


def middle_part(scale, last, info, got, other, den, factor):
    rows, cols = den.shape
    depth = factor.shape[1]
    vmem = pl.BlockSpec(memory_space=pltpu.VMEM)
    short = pltpu.VMEM((rows, depth), jnp.bfloat16)
    tall = pltpu.VMEM((cols, depth), jnp.bfloat16)
    wide = pltpu.VMEM((rows, cols), jnp.bfloat16)
    return pl.pallas_call(
        lambda *refs: middle_kernel(scale, last, *refs),
        out_shape=jax.ShapeDtypeStruct((rows, cols if last else depth), jnp.float32),
        in_specs=[pl.BlockSpec(memory_space=pltpu.SMEM), vmem, vmem, vmem, vmem],
        out_specs=vmem,
        scratch_shapes=[short, short, tall, tall, wide, wide],
        compiler_params=pltpu.CompilerParams(vmem_limit_bytes=20 << 20),
        cost_estimate=pl.CostEstimate(flops=12 * rows * depth * cols, bytes_accessed=4 << 20, transcendentals=0),
        name="last" if last else "middle",
    )(info, got, other, den, factor)


def local(amplitudes, factor, denominators):
    rows, depth = amplitudes.shape[0], factor.shape[1]
    nrow = lax.axis_size("row")
    ncol = lax.axis_size("col")
    line = ncol // PAIR
    thin = rows // ncol
    here_row = lax.axis_index("row")
    here_col = lax.axis_index("col")
    first = here_row % CORES == 0
    scale = 1.0 / math.sqrt(rows * nrow)
    info = jnp.stack([here_row % CORES, here_row // CORES == here_col]).astype(jnp.int32)
    team = [[k * CORES + e for e in range(CORES)] for k in range(ncol)]
    partner = [(r, r ^ 1) for r in range(nrow)]
    order = []
    for u in range(PAIR):
        for n in range(line):
            y = (n // 2 + (n + u) % 2 * (line // 2)) % line
            order.append(y * PAIR + u)
    place = [(c // PAIR + line // 2) % line * PAIR + c % PAIR for c in order]
    turn = [[] for _ in range(CORES)]
    for e in range(CORES):
        for c, q in zip(order, place):
            for k in range(ncol):
                turn[e].append(((k * CORES + e) * ncol + c, (q * CORES + 1) * ncol + k))
    both = [[k * CORES * ncol + c for c in order] for k in range(ncol)]
    both += [[(q * CORES + 1) * ncol + c for q in place] for c in range(ncol)]
    mine = lax.dynamic_slice_in_dim(factor, info[0] * rows, rows, 0)
    part = jnp.dot(amplitudes, factor, precision=lax.Precision.HIGH) * scale + jnp.where(info[1] == 1, mine, 0.0)
    for step in range(ITERS):
        terms = spread(part, "col", [order])
        piece = terms.reshape(ncol, thin, depth).sum(0)
        turned = []
        for e in range(CORES):
            turned.append(lax.ppermute(piece, ("row", "col"), turn[e]))
        pieces = lax.all_gather(piece, "row", axis=0, axis_index_groups=team, tiled=True)
        own = jnp.where(first, pieces, jnp.concatenate(turned))
        got = spread(jnp.tile(own, (ncol, 1)), ("row", "col"), both)
        other = lax.ppermute(got, "row", partner)
        got = got.reshape(ncol, CORES, thin, depth)
        other = other.reshape(ncol, CORES, thin, depth)
        part = middle_part(scale, step == ITERS - 1, info, got, other, denominators, factor)
    return part


def solution(mesh):
    return jax.shard_map(
        local,
        mesh=mesh,
        in_specs=(P("row", "col"), P("col", None), P("row", "col")),
        out_specs=P("row", "col"),
        check_vma=False,
    )
```

```python
import math

import jax
import jax.numpy as jnp
from jax import lax
from jax.experimental import pallas as pl
from jax.experimental.pallas import tpu as pltpu
from jax.sharding import PartitionSpec as P

ITERS = 2
WIDE = 256
PAIR = 2
CORES = 2


def spread(block, axis, groups):
    return lax.all_to_all(block, axis, split_axis=0, concat_axis=0, axis_index_groups=groups, tiled=True)


def halves(x):
    high = x.astype(jnp.bfloat16)
    return high, (x - high.astype(jnp.float32)).astype(jnp.bfloat16)


def product(left, right, transposed):
    dims = (((1,), (1 if transposed else 0,)), ((), ()))

    def dot(a, b):
        return lax.dot_general(a, b, dims, preferred_element_type=jnp.float32)

    return dot(left[0], right[0]) + (dot(left[0], right[1]) + dot(left[1], right[0]))


def middle_kernel(scale, last, info, got, other, den, factor, out, rh, rl, ch, cl, *more):
    rows, thin = out.shape[0], got.shape[2]

    def sort(cols, mine, e):
        for j in range(got.shape[0]):
            here = slice(j * thin, (j + 1) * thin)
            rh[here, :], rl[here, :] = halves(mine[j, e])
            for f in range(CORES):
                there = slice(f * rows + j * thin, f * rows + (j + 1) * thin)
                ch[there, :], cl[there, :] = halves(cols[j, f])

    @pl.when(info[0] == 0)
    def _():
        sort(other, got, 0)

    @pl.when(info[0] == 1)
    def _():
        sort(got, other, 1)

    if last:
        held, sems = more
        half = rows // 2
        right = ch[...], cl[...]
        stores = []
        for n in range(2):
            here = slice(n * half, (n + 1) * half)
            held[here, :] = product((rh[here, :], rl[here, :]), right, True) / den[here, :]
            stores.append(pltpu.make_async_copy(held.at[here, :], out.at[here, :], sems.at[n]))
            stores[n].start()
        for store in stores:
            store.wait()
    else:
        ah, al = more
        left = rh[...], rl[...]
        for at in range(0, ch.shape[0], WIDE):
            cols = slice(at, at + WIDE)
            ah[:, cols], al[:, cols] = halves(product(left, (ch[cols, :], cl[cols, :]), True) / den[:, cols])
    if not last:
        left = ah[...], al[...]
        for at in range(0, out.shape[1], WIDE):
            cols = slice(at, at + WIDE)
            out[:, cols] = product(left, halves(factor[:, cols]), False) * scale

        @pl.when(info[1] == 1)
        def _():
            out[...] += factor[pl.ds(pl.multiple_of(info[0] * rows, rows), rows), :]


def middle_part(scale, last, info, got, other, den, factor):
    rows, cols = den.shape
    depth = factor.shape[1]
    vmem = pl.BlockSpec(memory_space=pltpu.VMEM)
    short = pltpu.VMEM((rows, depth), jnp.bfloat16)
    tall = pltpu.VMEM((cols, depth), jnp.bfloat16)
    wide = pltpu.VMEM((rows, cols), jnp.bfloat16)
    more = [pltpu.VMEM((rows, cols), jnp.float32), pltpu.SemaphoreType.DMA((2,))] if last else [wide, wide]
    return pl.pallas_call(
        lambda *refs: middle_kernel(scale, last, *refs),
        out_shape=jax.ShapeDtypeStruct((rows, cols if last else depth), jnp.float32),
        in_specs=[pl.BlockSpec(memory_space=pltpu.SMEM), vmem, vmem, vmem, vmem],
        out_specs=pl.BlockSpec(memory_space=pl.ANY) if last else vmem,
        scratch_shapes=[short, short, tall, tall, *more],
        compiler_params=pltpu.CompilerParams(vmem_limit_bytes=20 << 20),
        cost_estimate=pl.CostEstimate(flops=12 * rows * depth * cols, bytes_accessed=4 << 20, transcendentals=0),
        name="last" if last else "middle",
    )(info, got, other, den, factor)


def local(amplitudes, factor, denominators):
    rows, depth = amplitudes.shape[0], factor.shape[1]
    nrow = lax.axis_size("row")
    ncol = lax.axis_size("col")
    line = ncol // PAIR
    thin = rows // ncol
    here_row = lax.axis_index("row")
    here_col = lax.axis_index("col")
    first = here_row % CORES == 0
    scale = 1.0 / math.sqrt(rows * nrow)
    info = jnp.stack([here_row % CORES, here_row // CORES == here_col]).astype(jnp.int32)
    team = [[k * CORES + e for e in range(CORES)] for k in range(ncol)]
    partner = [(r, r ^ 1) for r in range(nrow)]
    order = [y * PAIR + u for u in range(PAIR) for y in range(line)]
    place = [(c // PAIR + line // 2) % line * PAIR + c % PAIR for c in order]
    turn = [[] for _ in range(CORES)]
    for e in range(CORES):
        for c, q in zip(order, place):
            for k in range(ncol):
                turn[e].append(((k * CORES + e) * ncol + c, (q * CORES + 1) * ncol + k))
    both = [[k * CORES * ncol + c for c in order] for k in range(ncol)]
    both += [[(q * CORES + 1) * ncol + c for q in place] for c in range(ncol)]
    mine = lax.dynamic_slice_in_dim(factor, info[0] * rows, rows, 0)
    part = jnp.dot(amplitudes, factor, precision=lax.Precision.HIGH) * scale + jnp.where(info[1] == 1, mine, 0.0)
    for step in range(ITERS):
        terms = spread(part, "col", [order])
        piece = terms.reshape(ncol, thin, depth).sum(0)
        turned = []
        for e in range(CORES):
            turned.append(lax.ppermute(piece, ("row", "col"), turn[e]))
        pieces = lax.all_gather(piece, "row", axis=0, axis_index_groups=team, tiled=True)
        own = jnp.where(first, pieces, jnp.concatenate(turned))
        got = spread(jnp.tile(own, (ncol, 1)), ("row", "col"), both)
        other = lax.ppermute(got, "row", partner)
        got = got.reshape(ncol, CORES, thin, depth)
        other = other.reshape(ncol, CORES, thin, depth)
        part = middle_part(scale, step == ITERS - 1, info, got, other, denominators, factor)
    return part


def solution(mesh):
    return jax.shard_map(
        local,
        mesh=mesh,
        in_specs=(P("row", "col"), P("col", None), P("row", "col")),
        out_specs=P("row", "col"),
        check_vma=False,
    )
```

```python
import math

import jax
import jax.numpy as jnp
from jax import lax
from jax.experimental import pallas as pl
from jax.experimental.pallas import tpu as pltpu
from jax.sharding import PartitionSpec as P

ITERS = 2
WIDE = 512
PAIR = 2
CORES = 2


def spread(block, axis, groups):
    return lax.all_to_all(block, axis, split_axis=0, concat_axis=0, axis_index_groups=groups, tiled=True)


def halves(x):
    high = x.astype(jnp.bfloat16)
    return high, (x - high.astype(jnp.float32)).astype(jnp.bfloat16)


def product(left, right, transposed):
    dims = (((1,), (1 if transposed else 0,)), ((), ()))

    def dot(a, b):
        return lax.dot_general(a, b, dims, preferred_element_type=jnp.float32)

    return dot(left[0], right[0]) + (dot(left[0], right[1]) + dot(left[1], right[0]))


def middle_kernel(scale, last, info, got, other, den, factor, out, rh, rl, ch, cl, ah, al):
    rows, thin = out.shape[0], got.shape[2]

    def sort(cols, mine, e):
        for j in range(got.shape[0]):
            here = slice(j * thin, (j + 1) * thin)
            rh[here, :], rl[here, :] = halves(mine[j, e])
            for f in range(CORES):
                there = slice(f * rows + j * thin, f * rows + (j + 1) * thin)
                ch[there, :], cl[there, :] = halves(cols[j, f])

    @pl.when(info[0] == 0)
    def _():
        sort(other, got, 0)

    @pl.when(info[0] == 1)
    def _():
        sort(got, other, 1)

    left = rh[...], rl[...]
    for at in range(0, ch.shape[0], WIDE):
        cols = slice(at, at + WIDE)
        amp = product(left, (ch[cols, :], cl[cols, :]), True) / den[:, cols]
        if last:
            out[:, cols] = amp
        else:
            ah[:, cols], al[:, cols] = halves(amp)
    if not last:
        left = ah[...], al[...]
        for at in range(0, out.shape[1], WIDE):
            cols = slice(at, at + WIDE)
            out[:, cols] = product(left, halves(factor[:, cols]), False) * scale

        @pl.when(info[1] == 1)
        def _():
            out[...] += factor[pl.ds(pl.multiple_of(info[0] * rows, rows), rows), :]


def middle_part(scale, last, info, got, other, den, factor):
    rows, cols = den.shape
    depth = factor.shape[1]
    vmem = pl.BlockSpec(memory_space=pltpu.VMEM)
    short = pltpu.VMEM((rows, depth), jnp.bfloat16)
    tall = pltpu.VMEM((cols, depth), jnp.bfloat16)
    wide = pltpu.VMEM((rows, cols), jnp.bfloat16)
    return pl.pallas_call(
        lambda *refs: middle_kernel(scale, last, *refs),
        out_shape=jax.ShapeDtypeStruct((rows, cols if last else depth), jnp.float32),
        in_specs=[pl.BlockSpec(memory_space=pltpu.SMEM), vmem, vmem, vmem, vmem],
        out_specs=vmem,
        scratch_shapes=[short, short, tall, tall, wide, wide],
        compiler_params=pltpu.CompilerParams(vmem_limit_bytes=20 << 20),
        cost_estimate=pl.CostEstimate(flops=12 * rows * depth * cols, bytes_accessed=4 << 20, transcendentals=0),
        name="last" if last else "middle",
    )(info, got, other, den, factor)


def local(amplitudes, factor, denominators):
    rows, depth = amplitudes.shape[0], factor.shape[1]
    nrow = lax.axis_size("row")
    ncol = lax.axis_size("col")
    line = ncol // PAIR
    thin = rows // ncol
    here_row = lax.axis_index("row")
    here_col = lax.axis_index("col")
    first = here_row % CORES == 0
    scale = 1.0 / math.sqrt(rows * nrow)
    info = jnp.stack([here_row % CORES, here_row // CORES == here_col]).astype(jnp.int32)
    team = [[k * CORES + e for e in range(CORES)] for k in range(ncol)]
    partner = [(r, r ^ 1) for r in range(nrow)]
    order = [y * PAIR + u for u in range(PAIR) for y in range(line)]
    place = [(c // PAIR + line // 2) % line * PAIR + c % PAIR for c in order]
    turn = [[] for _ in range(CORES)]
    for e in range(CORES):
        for c, q in zip(order, place):
            for k in range(ncol):
                turn[e].append(((k * CORES + e) * ncol + c, (q * CORES + 1) * ncol + k))
    both = [[k * CORES * ncol + c for c in order] for k in range(ncol)]
    both += [[(q * CORES + 1) * ncol + c for q in place] for c in range(ncol)]
    mine = lax.dynamic_slice_in_dim(factor, info[0] * rows, rows, 0)
    part = jnp.dot(amplitudes, factor, precision=lax.Precision.HIGH) * scale + jnp.where(info[1] == 1, mine, 0.0)
    for step in range(ITERS):
        terms = spread(part, "col", [order])
        piece = terms.reshape(ncol, thin, depth).sum(0)
        turned = []
        for e in range(CORES):
            turned.append(lax.ppermute(piece, ("row", "col"), turn[e]))
        pieces = lax.all_gather(piece, "row", axis=0, axis_index_groups=team, tiled=True)
        own = jnp.where(first, pieces, jnp.concatenate(turned))
        got = spread(jnp.tile(own, (ncol, 1)), ("row", "col"), both)
        other = lax.ppermute(got, "row", partner)
        got = got.reshape(ncol, CORES, thin, depth)
        other = other.reshape(ncol, CORES, thin, depth)
        part = middle_part(scale, step == ITERS - 1, info, got, other, denominators, factor)
    return part


def solution(mesh):
    return jax.shard_map(
        local,
        mesh=mesh,
        in_specs=(P("row", "col"), P("col", None), P("row", "col")),
        out_specs=P("row", "col"),
        check_vma=False,
    )
```
